32 devices in a mesh: seq: 8 (over z, y), wsh: 4 (over x, core).
Axes of the slice: x: 2, y: 2, z: 4, core: 2. Of those that a mesh axis runs over, the one named last changes fastest.
Arguments:
- layer_input: bfloat16 [4096, 1152], P(('seq', 'wsh')), may hold values from -6 to 6
- w_qkv: bfloat16 [1152, 1536], P('wsh'), may hold values from -0.1875 to 0.1875
- w_out: bfloat16 [1152, 1024], P('wsh'), may hold values from -0.1875 to 0.1875
- w_gate_up: bfloat16 [1152, 6912], P('wsh'), may hold values from -0.1875 to 0.1875
- w_down: bfloat16 [1152, 3456], P('wsh'), may hold values from -0.109375 to 0.109375
- norm_gain: bfloat16 [4, 1152], P(None, 'wsh'), may hold values from 0.099609375 to 1.8984375
- qk_gain: bfloat16 [512], P('wsh'), may hold values from 0.099609375 to 1.8984375
- cotangent: bfloat16 [4096, 1152], P(('seq', 'wsh')), may hold values from -6 to 6
Outputs:
- output: bfloat16 [4096, 1152], P(('seq', 'wsh'))
- grad_input: float32 [4096, 1152], P(('seq', 'wsh'))
- grad_w_qkv: float32 [1152, 1536], P('wsh')
- grad_w_out: float32 [1152, 1024], P('wsh')
- grad_w_gate_up: float32 [1152, 6912], P('wsh')
- grad_w_down: float32 [1152, 3456], P('wsh')
- grad_norm_gain: float32 [4, 1152], P(None, 'wsh')
- grad_qk_gain: float32 [512], P('wsh')
The draws below stay inside these ranges and needn't reach their ends.
All inputs are finite; a program needn't handle non-finite values.
Results may differ from the reference program's by a relative error of at most 0.024.
Values may be sent and summed in bfloat16 or wider, within the bound.
No kernel may reach another device: no remote copies, remote signals or barrier semaphores. Data moves between devices by JAX's collectives and lax.ppermute only.
A program may use at most 192 MiB of HBM per device.

```python
import jax
import jax.numpy as jnp
from jax import lax

D = 1152
HQ = 4
HD = 256
WIN = 512
FF = 3456
QKV = 1536
BLOCK = 512
LENGTH = 4096
N_SEQ = 8


def shard_levels(stream_key, extent, cuts, smallest, top_value):
    factor_of = 1.0
    for dim, shards_of in cuts:
        draws = jax.random.uniform(jax.random.fold_in(jax.random.fold_in(stream_key, 6), dim), (shards_of,), jnp.float32, smallest / len(cuts), top_value / len(cuts))
        factor_of = factor_of * jnp.repeat(jnp.exp(draws), extent[dim] // shards_of).reshape((-1,) + (1,) * (len(extent) - 1 - dim))
    return factor_of


def centred(own_key, extent, width, bound, cuts=(), kind=jnp.bfloat16):
    entries = width * jax.random.normal(own_key, extent, jnp.float32)
    if cuts:
        entries = entries * shard_levels(own_key, extent, cuts, -0.22, 0.18)
    return jnp.clip(entries, -bound, bound).astype(kind)


def setup_inputs(seed: int = 0) -> dict:
    seeds = jax.random.split(jax.random.key(seed), 9)
    layer_input = centred(seeds[0], (LENGTH, D), 1.0, 6.0, ((0, 32),))
    w_qkv = centred(seeds[1], (D, QKV), D ** -0.5, 0.1875, ((0, 4),))
    w_out = centred(seeds[2], (D, HQ * HD), (HQ * HD) ** -0.5, 0.1875, ((0, 4),))
    w_gate_up = centred(seeds[3], (D, 2 * FF), D ** -0.5, 0.1875, ((0, 4),))
    w_down = centred(seeds[4], (D, FF), FF ** -0.5, 0.109375, ((0, 4),))
    norm_gain = jnp.clip(1.0 + 0.18 * jax.random.normal(seeds[5], (4, D), jnp.float32), 0.099609375, 1.8984375).astype(jnp.bfloat16)
    qk_gain = jnp.clip(1.0 + 0.18 * jax.random.normal(seeds[6], (2 * HD,), jnp.float32), 0.099609375, 1.8984375).astype(jnp.bfloat16)
    cotangent = centred(seeds[7], (LENGTH, D), 1.0, 6.0, ((0, 32),))
    return {"layer_input": layer_input, "w_qkv": w_qkv, "w_out": w_out, "w_gate_up": w_gate_up, "w_down": w_down, "norm_gain": norm_gain, "qk_gain": qk_gain, "cotangent": cotangent}


EPSILON = 1e-06
GELU_COEF = 0.7978845608028654

def gelu_tanh(values):
    return 0.5 * values * (1.0 + jnp.tanh(GELU_COEF * (values + 0.044715 * values * values * values)))

def gelu_slope(values):
    bend = jnp.tanh(GELU_COEF * (values + 0.044715 * values * values * values))
    return 0.5 * (1.0 + bend) + 0.5 * values * (1.0 - bend * bend) * GELU_COEF * (1.0 + 3.0 * 0.044715 * values * values)

def inv_rms(values):
    return lax.rsqrt(lax.optimization_barrier(jnp.mean(values * values, -1, keepdims=True)) + EPSILON)

def norm_back(grad_out, values, scale, gain):
    normed = values * scale
    scaled = grad_out * gain
    grad_in = scale * (scaled - normed * lax.optimization_barrier(jnp.mean(scaled * normed, -1, keepdims=True)))
    return (grad_in, grad_out * normed)

def rope_tables(positions, head_dim):
    half = head_dim // 2
    freqs = 10000.0 ** (-(jnp.arange(half, dtype=jnp.float32) * 2.0 / head_dim))
    angles = positions.astype(jnp.float32)[:, None] * freqs[None, :]
    cosine = jnp.cos(angles)
    sine = jnp.sin(angles)
    return (jnp.concatenate([cosine, cosine], -1), jnp.concatenate([sine, sine], -1))

def rotate(values, cosine, sine):
    half = values.shape[-1] // 2
    turned = jnp.concatenate([-values[..., half:], values[..., :half]], -1)
    return values * cosine + turned * sine

def unrotate(grads, cosine, sine):
    half = grads.shape[-1] // 2
    scaled = grads * sine
    turned = jnp.concatenate([scaled[..., half:], -scaled[..., :half]], -1)
    return grads * cosine + turned

def block_mask(query_pos, key_pos):
    gap = query_pos[:, None] - key_pos[None, :]
    return (gap >= 0) & (gap < WIN) & (key_pos[None, :] >= 0)

def rounded(values):
    return lax.optimization_barrier(values.astype(jnp.bfloat16)).astype(jnp.float32)

def scores_of(query_s, keys):
    head_dim = query_s.shape[-1]
    return jnp.einsum('qhd,kd->hqk', query_s.astype(jnp.float32), keys[:, :head_dim].astype(jnp.float32))

def attend(query_s, keys, mask):
    head_dim = query_s.shape[-1]
    scores = scores_of(query_s, keys)
    exps = jnp.where(mask[None], jnp.exp(scores), 0.0)
    total = lax.optimization_barrier(jnp.sum(exps, -1, keepdims=True))
    weights = rounded(exps / total)
    out = jnp.einsum('hqk,kd->qhd', weights, keys[:, head_dim:].astype(jnp.float32))
    return (out, jnp.log(total))

def attend_back(query_s, keys, mask, out, log_total, grad_out):
    head_dim = query_s.shape[-1]
    scores = scores_of(query_s, keys)
    probs = jnp.where(mask[None], jnp.exp(scores - log_total), 0.0)
    grad_float = grad_out.astype(jnp.float32)
    grad_prob = jnp.einsum('qhd,kd->hqk', grad_float, keys[:, head_dim:].astype(jnp.float32))
    delta = jnp.einsum('qhd,qhd->hq', grad_float, out)[:, :, None]
    grad_score = rounded(probs * (grad_prob - delta))
    grad_query = jnp.einsum('hqk,kd->qhd', grad_score, keys[:, :head_dim].astype(jnp.float32))
    grad_key = jnp.einsum('hqk,qhd->kd', grad_score, query_s.astype(jnp.float32))
    grad_value = jnp.einsum('hqk,qhd->kd', rounded(probs), grad_float)
    return (grad_query, jnp.concatenate([grad_key, grad_value], -1))

def reference(layer_input, w_qkv, w_out, w_gate_up, w_down, norm_gain, qk_gain, cotangent):
    gains = norm_gain.astype(jnp.float32)
    gain_query = qk_gain[:HD].astype(jnp.float32)
    gain_key = qk_gain[HD:].astype(jnp.float32)
    width_q = HQ * HD
    blocks_input = layer_input.reshape(N_SEQ, BLOCK, D)
    blocks_grad = cotangent.reshape(N_SEQ, BLOCK, D)
    starts = jnp.arange(N_SEQ, dtype=jnp.int32) * BLOCK

    def project(items):
        rows, start = items
        rows_f = rows.astype(jnp.float32)
        normed = (rows_f * inv_rms(rows_f) * gains[0]).astype(jnp.bfloat16)
        projected = jnp.dot(normed, w_qkv, preferred_element_type=jnp.float32)
        query = projected[:, :width_q].reshape(BLOCK, HQ, HD)
        key = projected[:, width_q:width_q + HD]
        value = projected[:, width_q + HD:]
        cosine, sine = rope_tables(start + jnp.arange(BLOCK, dtype=jnp.int32), HD)
        query_s = (rotate(query * inv_rms(query) * gain_query, cosine[:, None], sine[:, None]) * HD ** (-0.5)).astype(jnp.bfloat16)
        key_s = rotate(key * inv_rms(key) * gain_key, cosine, sine).astype(jnp.bfloat16)
        return (normed, query_s, jnp.concatenate([key_s, value.astype(jnp.bfloat16)], -1))
    normed_all, query_all, kv_all = lax.map(project, (blocks_input, starts))
    previous = jnp.concatenate([jnp.zeros((1, WIN, 2 * HD), jnp.bfloat16), kv_all[:-1, BLOCK - WIN:]], 0)
    keys_all = jnp.concatenate([previous, kv_all], 1)

    def middle(carry, items):
        acc_out, acc_gate_up, acc_down, acc_gains = carry
        rows, query_s, keys, start, grad_rows = items
        rows_f = rows.astype(jnp.float32)
        positions = start + jnp.arange(BLOCK, dtype=jnp.int32)
        key_pos = start - WIN + jnp.arange(WIN + BLOCK, dtype=jnp.int32)
        mask = block_mask(positions, key_pos)
        attended, log_total = attend(query_s, keys, mask)
        attended_b = attended.reshape(BLOCK, width_q).astype(jnp.bfloat16)
        branch = jnp.dot(attended_b, w_out.T, preferred_element_type=jnp.float32)
        scale2 = inv_rms(branch)
        hidden_res = rows_f + branch * scale2 * gains[1]
        scale3 = inv_rms(hidden_res)
        ffn_in = (hidden_res * scale3 * gains[2]).astype(jnp.bfloat16)
        gate_up = jnp.dot(ffn_in, w_gate_up, preferred_element_type=jnp.float32)
        gate = gate_up[:, :FF]
        upper = gate_up[:, FF:]
        mixed = (gelu_tanh(gate) * upper).astype(jnp.bfloat16)
        ffn_out = jnp.dot(mixed, w_down.T, preferred_element_type=jnp.float32)
        scale4 = inv_rms(ffn_out)
        output = (hidden_res + ffn_out * scale4 * gains[3]).astype(jnp.bfloat16)
        grad_y = grad_rows.astype(jnp.float32)
        grad_ffn, rows_three = norm_back(grad_y, ffn_out, scale4, gains[3])
        grad_ffn_b = grad_ffn.astype(jnp.bfloat16)
        grad_down_blk = jnp.dot(grad_ffn_b.T, mixed, preferred_element_type=jnp.float32)
        grad_mixed = jnp.dot(grad_ffn_b, w_down, preferred_element_type=jnp.float32)
        grad_gu = jnp.concatenate([grad_mixed * upper * gelu_slope(gate), grad_mixed * gelu_tanh(gate)], -1).astype(jnp.bfloat16)
        grad_gate_up_blk = jnp.dot(ffn_in.T, grad_gu, preferred_element_type=jnp.float32)
        grad_ffn_in = jnp.dot(grad_gu, w_gate_up.T, preferred_element_type=jnp.float32)
        grad_res, rows_two = norm_back(grad_ffn_in, hidden_res, scale3, gains[2])
        grad_hidden = grad_y + grad_res
        grad_branch, rows_one = norm_back(grad_hidden, branch, scale2, gains[1])
        grad_branch_b = grad_branch.astype(jnp.bfloat16)
        grad_out_blk = jnp.dot(grad_branch_b.T, attended_b, preferred_element_type=jnp.float32)
        grad_att = jnp.dot(grad_branch_b, w_out, preferred_element_type=jnp.float32).astype(jnp.bfloat16).reshape(BLOCK, HQ, HD)
        grad_query, grad_keys = attend_back(query_s, keys, mask, attended, log_total, grad_att)
        gain_sums = jnp.stack([lax.optimization_barrier(jnp.sum(rows_one, 0)), lax.optimization_barrier(jnp.sum(rows_two, 0)), lax.optimization_barrier(jnp.sum(rows_three, 0))])
        carry = (acc_out + grad_out_blk, acc_gate_up + grad_gate_up_blk, acc_down + grad_down_blk, acc_gains + gain_sums)
        return (carry, (output, grad_hidden, grad_query, grad_keys))
    init_mid = (jnp.zeros((D, width_q), jnp.float32), jnp.zeros((D, 2 * FF), jnp.float32), jnp.zeros((D, FF), jnp.float32), jnp.zeros((3, D), jnp.float32))
    (grad_w_out, grad_w_gate_up, grad_w_down, gains_late), (outputs, grad_hidden_all, grad_query_all, grad_keys_all) = lax.scan(middle, init_mid, (blocks_input, query_all, keys_all, starts, blocks_grad))
    own = grad_keys_all[:, WIN:]
    before = grad_keys_all[:, :WIN]
    carried = jnp.concatenate([before[1:], jnp.zeros((1, WIN, 2 * HD), jnp.float32)], 0)
    own = jnp.concatenate([own[:, :BLOCK - WIN], own[:, BLOCK - WIN:] + carried], 1)

    def front_back(carry, items):
        acc_qkv, acc_zero, acc_query, acc_key = carry
        rows, normed, start, grad_query, grad_kv, grad_hidden = items
        projected = jnp.dot(normed, w_qkv, preferred_element_type=jnp.float32)
        query = projected[:, :width_q].reshape(BLOCK, HQ, HD)
        key = projected[:, width_q:width_q + HD]
        cosine, sine = rope_tables(start + jnp.arange(BLOCK, dtype=jnp.int32), HD)
        grad_qn = unrotate(grad_query, cosine[:, None], sine[:, None]) * HD ** (-0.5)
        grad_q, rows_query = norm_back(grad_qn, query, inv_rms(query), gain_query)
        grad_kn = unrotate(grad_kv[:, :HD], cosine, sine)
        grad_k, rows_key = norm_back(grad_kn, key, inv_rms(key), gain_key)
        grad_qkv = jnp.concatenate([grad_q.reshape(BLOCK, width_q), grad_k, grad_kv[:, HD:]], -1).astype(jnp.bfloat16)
        grad_qkv_blk = jnp.dot(normed.T, grad_qkv, preferred_element_type=jnp.float32)
        grad_normed = jnp.dot(grad_qkv, w_qkv.T, preferred_element_type=jnp.float32)
        rows_f = rows.astype(jnp.float32)
        grad_in, rows_zero = norm_back(grad_normed, rows_f, inv_rms(rows_f), gains[0])
        carry = (acc_qkv + grad_qkv_blk, acc_zero + lax.optimization_barrier(jnp.sum(rows_zero, 0)), acc_query + lax.optimization_barrier(jnp.sum(rows_query, (0, 1))), acc_key + lax.optimization_barrier(jnp.sum(rows_key, 0)))
        return (carry, grad_hidden + grad_in)
    init_front = (jnp.zeros((D, QKV), jnp.float32), jnp.zeros((D,), jnp.float32), jnp.zeros((HD,), jnp.float32), jnp.zeros((HD,), jnp.float32))
    (grad_w_qkv, gain_zero, gain_q_sum, gain_k_sum), grad_in_blocks = lax.scan(front_back, init_front, (blocks_input, normed_all, starts, grad_query_all, own, grad_hidden_all))
    grad_norm_gain = jnp.concatenate([gain_zero[None], gains_late], 0)
    grad_qk_gain = jnp.concatenate([gain_q_sum, gain_k_sum], 0)
    return (outputs.reshape(LENGTH, D), grad_in_blocks.reshape(LENGTH, D), grad_w_qkv, grad_w_out, grad_w_gate_up, grad_w_down, grad_norm_gain, grad_qk_gain)
```

```python
import jax
import jax.numpy as jnp
from jax import lax
from jax.sharding import PartitionSpec as P

WIN = 512


EPSILON = 1e-06
GELU_COEF = 0.7978845608028654
LANES = 128
GATES = (1, 2, 3)


def gelu_parts(values):
    bend = jnp.tanh(GELU_COEF * (values + 0.044715 * values * values * values))
    value = 0.5 * values * (1.0 + bend)
    slope = 0.5 * (1.0 + bend) + 0.5 * values * (1.0 - bend * bend) * GELU_COEF * (
        1.0 + 3.0 * 0.044715 * values * values
    )
    return (value, slope)


def inv_rms(values):
    return lax.rsqrt(jnp.mean(values * values, -1, keepdims=True) + EPSILON)


def norm_back(grad_out, values, scale, gain):
    normed = values * scale
    scaled = grad_out * gain
    grad_in = scale * (scaled - normed * jnp.mean(scaled * normed, -1, keepdims=True))
    return (grad_in, grad_out * normed)


def rope_tables(positions, head_dim):
    half = head_dim // 2
    freqs = 10000.0 ** (-(jnp.arange(half, dtype=jnp.float32) * 2.0 / head_dim))
    angles = positions.astype(jnp.float32)[:, None] * freqs[None, :]
    cosine = jnp.cos(angles)
    sine = jnp.sin(angles)
    return (jnp.concatenate([cosine, cosine], -1), jnp.concatenate([sine, sine], -1))


def rotate(values, cosine, sine):
    half = values.shape[-1] // 2
    turned = jnp.concatenate([-values[..., half:], values[..., :half]], -1)
    return values * cosine + turned * sine


def unrotate(grads, cosine, sine):
    half = grads.shape[-1] // 2
    scaled = grads * sine
    turned = jnp.concatenate([scaled[..., half:], -scaled[..., :half]], -1)
    return grads * cosine + turned


def block_mask(query_pos, key_pos):
    gap = query_pos[:, None] - key_pos[None, :]
    return (gap >= 0) & (gap < WIN) & (key_pos[None, :] >= 0)


def dot(left, right, dims):
    return lax.dot_general(left, right, ((dims[0], dims[1]), ((), ())), preferred_element_type=jnp.float32)


def rows_by_cols(left, right):
    return dot(left, right, ((1,), (0,)))


def rows_by_rows(left, right):
    return dot(left, right, ((1,), (1,)))


def outer_sum(left, right):
    return dot(left, right, ((0,), (0,)))


def bf(values):
    return values.astype(jnp.bfloat16)


def attend(query_s, keys, mask):
    head_dim = query_s.shape[-1]
    scores = jnp.einsum(
        "qhd,kd->hqk", query_s, keys[:, :head_dim], preferred_element_type=jnp.float32
    )
    exps = jnp.where(mask[None], jnp.exp(scores), 0.0)
    total = jnp.sum(exps, -1, keepdims=True)
    weights = (exps / total).astype(jnp.bfloat16)
    out = jnp.einsum("hqk,kd->qhd", weights, keys[:, head_dim:], preferred_element_type=jnp.float32)
    return (out, jnp.log(total))


def attend_back(query_s, keys, mask, out, log_total, grad_out):
    head_dim = query_s.shape[-1]
    scores = jnp.einsum(
        "qhd,kd->hqk", query_s, keys[:, :head_dim], preferred_element_type=jnp.float32
    )
    probs = jnp.where(mask[None], jnp.exp(scores - log_total), 0.0)
    grad_prob = jnp.einsum(
        "qhd,kd->hqk", grad_out, keys[:, head_dim:], preferred_element_type=jnp.float32
    )
    delta = jnp.einsum("qhd,qhd->hq", grad_out.astype(jnp.float32), out)[:, :, None]
    grad_score = (probs * (grad_prob - delta)).astype(jnp.bfloat16)
    grad_query = jnp.einsum(
        "hqk,kd->qhd", grad_score, keys[:, :head_dim], preferred_element_type=jnp.float32
    )
    grad_key = jnp.einsum("hqk,qhd->kd", grad_score, query_s, preferred_element_type=jnp.float32)
    grad_value = jnp.einsum(
        "hqk,qhd->kd", probs.astype(jnp.bfloat16), grad_out, preferred_element_type=jnp.float32
    )
    return (grad_query, jnp.concatenate([grad_key, grad_value], -1))


def swap(value, bits, axis="wsh"):
    return lax.ppermute(value, axis, [(i, i ^ bits) for i in range(lax.axis_size(axis))])


def bits_of(axis):
    size = lax.axis_size(axis)
    return [1 << k for k in range(size.bit_length() - 1)]


def gather_parts(value):
    parts = {0: value}
    for bit in reversed(bits_of("wsh")):
        parts.update({offset ^ bit: swap(part, bit) for offset, part in list(parts.items())})
    return [parts[offset] for offset in range(lax.axis_size("wsh"))]


def exchange_parts(pieces, me):
    return [
        (lambda piece: piece if offset == 0 else swap(piece, offset))(
            lax.dynamic_index_in_dim(pieces, me ^ offset, 0, keepdims=False)
        )
        for offset in range(lax.axis_size("wsh"))
    ]


def after(value, *others):
    return lax.optimization_barrier((value,) + others)[0]


def far_swap(piece, bits, relayed):
    rows = piece.shape[0]
    if lax.axis_size("seq") % 2 or not relayed:
        return [(0, swap(piece, bits))]
    parity = lax.axis_index("seq") % 2
    mine = parity * relayed
    near = swap(lax.dynamic_slice_in_dim(piece, mine, relayed, 0), bits)
    got = [(mine, near)]
    if 2 * relayed < rows:
        got.append((2 * relayed, swap(piece[2 * relayed :], bits)))
    got.append((relayed - mine, swap(near, 1, "seq")))
    return got


def place_rows(pieces, rows, me, dtype):
    whole = jnp.zeros((rows * lax.axis_size("wsh"), pieces[0][2].shape[1]), dtype)
    for offset, first, piece in pieces:
        whole = lax.dynamic_update_slice(whole, piece, ((me ^ offset) * rows + first, 0))
    return whole


def gather_rows(shard, me, relayed):
    rows = shard.shape[0]
    pieces = [(0, 0, shard), (1, 0, swap(shard, 1))]
    for bits in range(2, lax.axis_size("wsh"), 2):
        for first, piece in far_swap(shard, bits, relayed):
            pieces += [(bits, first, piece), (bits ^ 1, first, swap(piece, 1))]
    return place_rows(pieces, rows, me, shard.dtype)


def in_order(parts, me):
    whole = jnp.zeros((len(parts),) + parts[0].shape, parts[0].dtype)
    for offset, part in enumerate(parts):
        whole = lax.dynamic_update_index_in_dim(whole, part, me ^ offset, 0)
    return whole


def reduce_parts(total):
    count = lax.axis_size("wsh")
    parts = dict(enumerate(jnp.split(total, count, 0)))
    for bit in bits_of("wsh"):
        kept = [offset for offset in parts if not offset & bit]
        sent = jnp.concatenate([bf(parts[offset ^ bit]) for offset in kept], 0)
        got = jnp.split(swap(sent, bit), len(kept), 0)
        parts = {offset: parts[offset] + part for offset, part in zip(kept, got)}
    return parts[0]


def column_piece(matrices, width, which):
    parts = []
    for matrix in matrices:
        columns = matrix.shape[1]
        piece = None
        for k in range(lax.axis_size("wsh")):
            each = matrix[:, min(k * width, columns) : min((k + 1) * width, columns)]
            each = jnp.pad(each, ((0, 0), (0, width - each.shape[1])))
            piece = each if piece is None else jnp.where(which == k, each, piece)
        parts.append(piece)
    return jnp.concatenate(parts, 1) if len(parts) > 1 else parts[0]


def column_pieces(matrix, width):
    count = lax.axis_size("wsh")
    return jnp.stack([matrix[:, k * width : (k + 1) * width] for k in range(count)])


def hidden_shards(w_gate_up, w_down, width, me, gate):
    count = lax.axis_size("wsh")
    size = lax.axis_size("seq")
    rows, hidden_units = w_down.shape

    def pieces_of(w_gate_up, w_down, which):
        return column_piece(
            (w_gate_up[:, :hidden_units], w_gate_up[:, hidden_units:], w_down), width, which
        )

    far = count - 2
    spread = far * rows % size == 0 and rows % (far * rows // size) == 0
    if spread:
        each = far * rows // size
        index = lax.axis_index("seq")
        per = size // far
        first = (index % per) * each
        sent = pieces_of(
            lax.dynamic_slice_in_dim(w_gate_up, first, each, 0),
            lax.dynamic_slice_in_dim(w_down, first, each, 0),
            me ^ (2 + index // per),
        )
        pairs = [
            (s * count + w, s * count + (w ^ (2 + s // per)))
            for s in range(size)
            for w in range(count)
        ]
        got = lax.ppermute(sent, ("seq", "wsh"), pairs)
        got = lax.all_gather(got, "seq", axis=0, tiled=True)
        distant = [got[k * rows : (k + 1) * rows] for k in range(far)]
    else:
        distant = [swap(pieces_of(w_gate_up, w_down, me ^ k), k) for k in range(2, count)]
    w_gate_up, w_down = (after(each, gate) for each in (w_gate_up, w_down))
    pieces = [pieces_of(w_gate_up, w_down, me), swap(pieces_of(w_gate_up, w_down, me ^ 1), 1)]
    pieces += distant
    return [
        place_rows([(k, 0, piece[:, lo:hi]) for k, piece in enumerate(pieces)], rows, me, w_down.dtype)
        for lo, hi in ((0, 2 * width), (2 * width, 3 * width))
    ]


def ring_order():
    size = lax.axis_size("seq")
    order = list(range(0, size, 2)) + list(range(size - 1 - size % 2, 0, -2))
    forward = [(order[i], order[(i + 1) % size]) for i in range(size)]
    index = lax.axis_index("seq")
    place = jnp.where(index % 2 == 0, index // 2, size - 1 - index // 2)
    return (size, place, forward, [(b, a) for a, b in forward])


def core_swap(shard, me):
    half = lax.axis_size("wsh") // 2
    rows = shard.shape[0] // (2 * half)
    view = bf(shard).reshape(half, 2, rows, shard.shape[1])
    other = swap(lax.dynamic_index_in_dim(view, 1 - me % 2, 1, keepdims=False), 1)
    return (view, other)


def far_pieces(sums, me):
    stacked = jnp.stack(sums)
    far = me // 2
    held = [lax.dynamic_index_in_dim(stacked, far, 0, keepdims=False)]
    for offset in range(1, len(sums)):
        piece = lax.dynamic_index_in_dim(stacked, far ^ offset, 0, keepdims=False)
        held.append(swap(piece, 2 * offset))
    return held


def put(outs, layout, part, offset, chunk, me):
    bands = lax.axis_size("seq") // 2
    step_rows = part.shape[0]
    source = 2 * ((me // 2) ^ offset) + ((me % 2) ^ (chunk // bands))
    first = (chunk % bands) * step_rows
    done = []
    start = 0
    for out, width in zip(outs, layout):
        piece = part[:, start : start + width]
        done.append(lax.dynamic_update_slice(out, piece, (first, source * width)))
        start += width
    return done


def empty_outs(rows, layout):
    count = lax.axis_size("wsh")
    return [jnp.zeros((rows, count * width), jnp.bfloat16) for width in layout]


def plain_sums(shard, layout, me):
    count = lax.axis_size("wsh")
    rows = shard.shape[0] // count
    parts = exchange_parts(bf(shard).reshape(count, rows, shard.shape[1]), me)
    parts = lax.psum(jnp.stack(parts), "seq").astype(jnp.float32)
    outs = empty_outs(rows, layout)
    for offset in range(count):
        start = 0
        for which, width in enumerate(layout):
            piece = bf(parts[offset, :, start : start + width])
            outs[which] = lax.dynamic_update_slice(outs[which], piece, (0, (me ^ offset) * width))
            start += width
    return outs


def ring_fits():
    return lax.axis_size("seq") == 8 and lax.axis_size("wsh") == 4


def ring_sums(shards, layout, me):
    if not ring_fits():
        outs = plain_sums(jnp.concatenate(shards, 1), layout, me)
        return (outs, [outs[-1]] * 8)
    size, place, forward, backward = ring_order()
    half = lax.axis_size("wsh") // 2
    core = me % 2
    rows = shards[0].shape[0] // (2 * half)
    step_rows = rows * 2 // size
    ways = [(1, forward) if owner % 2 == 0 else (-1, backward) for owner in range(half)]
    view, other = core_swap(jnp.concatenate([bf(shard) for shard in shards], 1), me)
    width = view.shape[-1]

    def take(owner, chunk):
        chunk = chunk % size
        band = (chunk % (size // 2)) * step_rows
        mine = lax.dynamic_slice(view, (owner, core, band, 0), (1, 1, step_rows, width))
        theirs = lax.dynamic_slice(other, (owner, band, 0), (1, step_rows, width))
        shape = (step_rows, width)
        return jnp.where(chunk < size // 2, mine.reshape(shape), theirs.reshape(shape))

    sums = [take(owner, place - way + size) for owner, (way, _) in enumerate(ways)]
    marks = [sums[0]]
    for step in range(1, size):
        sums = [lax.ppermute(part, "seq", ways[k][1]) for k, part in enumerate(sums)]
        sums = [
            part + take(owner, place - ways[owner][0] * (1 + step) + 2 * size)
            for owner, part in enumerate(sums)
        ]
        sums = list(lax.optimization_barrier(tuple(sums)))
        marks.append(sums[0])
    held = far_pieces(sums, me)
    outs = empty_outs(rows, layout)
    for offset, part in enumerate(held):
        outs = put(outs, layout, part, offset, place, me)
    for step in range(1, size):
        held = [lax.ppermute(part, "seq", ways[k][1]) for k, part in enumerate(held)]
        for offset, part in enumerate(held):
            chunk = (place - ways[offset][0] * step + size) % size
            outs = put(outs, layout, part, offset, chunk, me)
    return (outs, marks)


def cube_sums(shard, layout, me):
    if not ring_fits():
        return plain_sums(shard, layout, me)
    size = lax.axis_size("seq")
    view, other = core_swap(shard, me)
    half, _, rows, width = view.shape
    mine = lax.dynamic_index_in_dim(view, me % 2, 1, keepdims=False)
    bits = bits_of("seq")
    value = jnp.stack([mine, other], 1).reshape(half, size, rows * 2 // size, width)
    place = lax.axis_index("seq")
    for bit in bits:
        value = value.reshape(half, value.shape[1] // 2, 2, rows * 2 // size, width)
        at = (place // bit) % 2
        sent = lax.dynamic_index_in_dim(value, 1 - at, 2, keepdims=False)
        kept = lax.dynamic_index_in_dim(value, at, 2, keepdims=False)
        value = kept + swap(sent, bit, "seq")
    held = jnp.stack(far_pieces([value[k, 0] for k in range(half)], me))[None]
    offsets = [0]
    for bit in reversed(bits):
        held = jnp.concatenate([held, swap(held, bit, "seq")], 0)
        offsets += [offset ^ bit for offset in offsets]
    result = empty_outs(rows, layout)
    for k, offset in enumerate(offsets):
        for far_offset in range(half):
            result = put(result, layout, held[k, far_offset], far_offset, place ^ offset, me)
    return result


def total_over_all(value):
    for axis in ("wsh", "seq"):
        for bit in bits_of(axis):
            value = value + swap(value, bit, axis)
    return value


def body(layer_input, w_qkv, w_out, w_gate_up, w_down, norm_gain, qk_gain, cotangent):
    wsh_count = lax.axis_size("wsh")
    seq_count = lax.axis_size("seq")
    seq_index = lax.axis_index("seq")
    me = lax.axis_index("wsh")
    rows, model = layer_input.shape
    own_model = model // wsh_count
    head_dim = qk_gain.shape[0] * wsh_count // 2
    width_q = w_out.shape[1]
    heads = width_q // head_dim
    hidden_units = w_down.shape[1]
    hidden_own = -(-hidden_units // (wsh_count * LANES)) * LANES
    reach = -(-WIN // rows)

    packed = jnp.concatenate([norm_gain.reshape(1, -1), qk_gain.reshape(1, -1)], 1)
    packed = in_order([packed if o == 0 else swap(packed, o) for o in range(wsh_count)], me)
    packed = packed.reshape(wsh_count, -1)
    gains = (
        packed[:, : 4 * own_model]
        .reshape(wsh_count, 4, own_model)
        .transpose(1, 0, 2)
        .reshape(4, model)
        .astype(jnp.float32)
    )
    qk_full = packed[:, 4 * own_model :].reshape(-1).astype(jnp.float32)
    gain_query = qk_full[:head_dim]
    gain_key = qk_full[head_dim:]

    shard_rows = w_qkv.shape[0]
    third = shard_rows // 3 if shard_rows % 24 == 0 else 0
    qkv_full = gather_rows(w_qkv, me, third)
    gate_up_own, down_own = hidden_shards(w_gate_up, w_down, hidden_own, me, w_qkv)
    out_full = gather_rows(w_out, me, 0)

    own_start = (seq_index * wsh_count + me) * rows
    positions = own_start + jnp.arange(rows, dtype=jnp.int32)
    key_pos = own_start - reach * rows + jnp.arange((reach + 1) * rows, dtype=jnp.int32)
    mask = block_mask(positions, key_pos)
    cosine, sine = rope_tables(positions, head_dim)
    rows_f = layer_input.astype(jnp.float32)
    scale1 = inv_rms(rows_f)
    normed = bf(rows_f * scale1 * gains[0])
    projected = rows_by_cols(normed, qkv_full)
    query = projected[:, :width_q].reshape(rows, heads, head_dim)
    key = projected[:, width_q : width_q + head_dim]
    value = projected[:, width_q + head_dim :]
    scale_q = inv_rms(query)
    scale_k = inv_rms(key)
    key_s = bf(rotate(key * scale_k * gain_key, cosine, sine))
    local_kv = jnp.concatenate([key_s, bf(value)], -1)
    query_s = bf(
        rotate(query * scale_q * gain_query, cosine[:, None], sine[:, None]) * head_dim ** (-0.5)
    )
    total = wsh_count * seq_count

    def shifted(value, by):
        pairs = [(i, (i + by) % total) for i in range(total)]
        return lax.ppermute(value, ("seq", "wsh"), pairs)

    keys = jnp.concatenate([shifted(local_kv, by) for by in range(reach, 0, -1)] + [local_kv], 0)
    attended, log_total = attend(query_s, keys, mask)
    attended_b = bf(attended.reshape(rows, width_q))
    branch = rows_by_rows(attended_b, out_full)
    scale2 = inv_rms(branch)
    hidden_res = rows_f + branch * scale2 * gains[1]
    scale3 = inv_rms(hidden_res)
    ffn_in = bf(hidden_res * scale3 * gains[2])

    block_in = jnp.concatenate(gather_parts(ffn_in), 0)
    gate_up = rows_by_cols(block_in, gate_up_own)
    gate = gate_up[:, :hidden_own]
    upper = gate_up[:, hidden_own:]
    gate_value, gate_slope = gelu_parts(gate)
    mixed = bf(gate_value * upper)
    ffn_out = reduce_parts(rows_by_rows(mixed, down_own))
    scale4 = inv_rms(ffn_out)
    output = bf(hidden_res + ffn_out * scale4 * gains[3])
    grad_y = cotangent.astype(jnp.float32)
    grad_ffn, rows_three = norm_back(grad_y, ffn_out, scale4, gains[3])
    block_grad = jnp.concatenate(gather_parts(bf(grad_ffn)), 0)
    grad_mixed = rows_by_cols(block_grad, down_own)
    grad_gu = jnp.concatenate(
        [bf(grad_mixed * upper * gate_slope), bf(grad_mixed * gate_value)], -1
    )
    grad_in_part = rows_by_rows(grad_gu, gate_up_own)
    grad_ffn_in = reduce_parts(grad_in_part)
    block_in = after(block_in, grad_in_part)
    block_grad = after(block_grad, grad_in_part)
    (grad_gate, grad_up, grad_down), marks = ring_sums(
        (outer_sum(block_in, grad_gu), outer_sum(block_grad, mixed)), (hidden_own,) * 3, me
    )
    grad_ffn_in = after(grad_ffn_in, marks[GATES[0]])

    grad_res, rows_two = norm_back(grad_ffn_in, hidden_res, scale3, gains[2])
    grad_hidden = grad_y + grad_res
    grad_branch, rows_one = norm_back(grad_hidden, branch, scale2, gains[1])
    grad_branch_b = bf(grad_branch)
    grad_att = bf(rows_by_cols(grad_branch_b, out_full)).reshape(rows, heads, head_dim)
    grad_query, grad_keys = attend_back(query_s, keys, mask, attended, log_total, grad_att)
    grad_keys = after(grad_keys, marks[GATES[1]])
    grad_parts = jnp.split(bf(grad_keys), reach + 1, 0)
    grad_kv = grad_keys[reach * rows :]
    for by in range(1, reach + 1):
        grad_kv = grad_kv + shifted(grad_parts[reach - by], -by).astype(jnp.float32)
    grad_kv = after(grad_kv, marks[GATES[2]])
    grad_qn = unrotate(grad_query, cosine[:, None], sine[:, None]) * head_dim ** (-0.5)
    grad_q, rows_query = norm_back(grad_qn, query, scale_q, gain_query)
    grad_kn = unrotate(grad_kv[:, :head_dim], cosine, sine)
    grad_k, rows_key = norm_back(grad_kn, key, scale_k, gain_key)
    grad_qkv = bf(
        jnp.concatenate([grad_q.reshape(rows, width_q), grad_k, grad_kv[:, head_dim:]], -1)
    )
    grad_normed = rows_by_rows(grad_qkv, qkv_full)
    grad_in, rows_zero = norm_back(grad_normed, rows_f, scale1, gains[0])
    grad_input = grad_hidden + grad_in

    out_width = width_q // wsh_count
    qkv_width = w_qkv.shape[1] // wsh_count
    block_branch = jnp.concatenate(gather_parts(grad_branch_b), 0)
    block_att = jnp.concatenate(exchange_parts(column_pieces(attended_b, out_width), me), 0)
    block_normed = jnp.concatenate(gather_parts(normed), 0)
    block_qkv = jnp.concatenate(exchange_parts(column_pieces(grad_qkv, qkv_width), me), 0)
    (grad_out,) = cube_sums(outer_sum(block_branch, block_att), (out_width,), me)
    (grad_w_qkv,) = cube_sums(outer_sum(block_normed, block_qkv), (qkv_width,), me)

    sums = jnp.concatenate(
        [jnp.sum(each, 0).reshape(1, model) for each in (rows_zero, rows_one, rows_two, rows_three)]
        + [jnp.sum(rows_query, (0, 1)).reshape(1, -1), jnp.sum(rows_key, 0).reshape(1, -1)],
        1,
    )
    sums = total_over_all(sums)
    gain_grads = lax.dynamic_index_in_dim(
        sums[:, : 4 * model].reshape(4, wsh_count, own_model), me, 1, keepdims=False
    )
    qk_grads = lax.dynamic_slice_in_dim(
        sums[0, 4 * model :], me * qk_gain.shape[0], qk_gain.shape[0], 0
    )
    return (
        output,
        grad_input,
        grad_w_qkv.astype(jnp.float32),
        grad_out.astype(jnp.float32),
        jnp.concatenate([grad_gate[:, :hidden_units], grad_up[:, :hidden_units]], 1).astype(
            jnp.float32
        ),
        grad_down[:, :hidden_units].astype(jnp.float32),
        gain_grads,
        qk_grads,
    )


def solution(mesh):
    in_specs = (
        P(("seq", "wsh"), None),
        P("wsh", None),
        P("wsh", None),
        P("wsh", None),
        P("wsh", None),
        P(None, "wsh"),
        P("wsh"),
        P(("seq", "wsh"), None),
    )
    out_specs = (
        P(("seq", "wsh"), None),
        P(("seq", "wsh"), None),
        P("wsh", None),
        P("wsh", None),
        P("wsh", None),
        P("wsh", None),
        P(None, "wsh"),
        P("wsh"),
    )
    return jax.shard_map(body, mesh=mesh, in_specs=in_specs, out_specs=out_specs, check_vma=False)
```
